32 devices in a mesh: row: 8 (over z, core), col: 4 (over y, x).
Axes of the slice: x: 2, y: 2, z: 4, core: 2. Of those that a mesh axis runs over, the one named last changes fastest.
Arguments:
- density_owned: float32 [8, 4, 4, 512, 512], P('row', 'col'), may hold values from -0.125 to 0.125
- hamilton_owned: float32 [8, 4, 3, 512, 512], P('row', 'col'), may hold values from -6 to 6
- density_route: int32 [8, 4, 4, 2], P('row', 'col'), may hold values from 0 to 7, as said below
- hamilton_route: int32 [8, 4, 3, 2], P('row', 'col'), may hold values from 0 to 7, as said below
- pair_lists: int32 [8, 4, 3, 12, 3], P('row', 'col'), may hold values from 0 to 5, as said below
- pair_counts: int32 [8, 4, 3], P('row', 'col'), may hold values from 4 to 12, as said below
Outputs:
- product: float32 [8, 4, 4, 512, 512], P('row', 'col')
The draws below stay inside these ranges and needn't reach their ends.
Inputs may be any that keep to these rules, and one draw needn't show every extreme that they name: `density_route`: entry (t, u): the grid row t in the owner's own grid column that takes the block and its slot u there. Every grid device takes exactly one density block for each of its 4 slots and one Hamiltonian block for each of its 3 slots, and the 7 blocks of one owner go to different grid rows. `hamilton_route`: as for density_route; the Hamiltonian slot u is below 3. `pair_lists`: entry (x, y, o): x below 4, y below 6, o below 4; the first 4 entries of each list name every product slot once. Only the first pair_counts[i, j, s] entries of list (i, j, s) count; at every stop some grid device has 12.
All inputs are finite; a program needn't handle non-finite values.
Results may differ from the reference program's by a relative error of at most 0.0003.
Values sent between devices are 32-bit elements; how exact they have to be, the bound alone decides.
No kernel may reach another device: no remote copies, remote signals or barrier semaphores. Data moves between devices by JAX's collectives and lax.ppermute only.
A program may use at most 128 MiB of HBM per device.

```python
import jax
import jax.numpy as jnp
from jax import lax

BS = 512
SA = 4
HB = 3
OUT = 4
PAIRS = 12
STOPS = 3
N_ROW = 8
N_COL = 4


def route_tables(key):
    offsets = jax.vmap(lambda inner: jax.random.permutation(inner, N_ROW)[:SA + HB])(jax.random.split(jax.random.fold_in(key, 11), N_COL))
    order_left = jax.vmap(lambda inner: jax.random.permutation(inner, SA))(jax.random.split(jax.random.fold_in(key, 12), N_ROW * N_COL)).reshape(N_ROW, N_COL, SA)
    order_right = jax.vmap(lambda inner: jax.random.permutation(inner, HB))(jax.random.split(jax.random.fold_in(key, 13), N_ROW * N_COL)).reshape(N_ROW, N_COL, HB)
    owner = jnp.arange(N_ROW, dtype=jnp.int32)[:, None, None]
    column = jnp.arange(N_COL, dtype=jnp.int32)[None, :, None]
    left_rows = (owner + offsets[column, order_left]) % N_ROW
    right_rows = (owner + offsets[column, SA + order_right]) % N_ROW
    left_route = jnp.stack([left_rows, order_left], axis=-1).astype(jnp.int32)
    right_route = jnp.stack([right_rows, order_right], axis=-1).astype(jnp.int32)
    return (left_route, right_route)


def draw_density_route(key, part):
    return route_tables(key)[0]


def draw_hamilton_route(key, part):
    return route_tables(key)[1]


def draw_pair_lists(key, part):
    first, second, third, fourth = jax.random.split(key, 4)
    shape = (N_ROW, N_COL, STOPS, PAIRS)
    left_slot = jax.random.randint(first, shape, 0, SA)
    right_slot = jax.random.randint(second, shape, 0, 2 * HB)
    spread = jax.random.randint(third, shape, 0, OUT)
    orders = jax.vmap(lambda inner: jax.random.permutation(inner, OUT))(jax.random.split(fourth, N_ROW * N_COL * STOPS)).reshape(N_ROW, N_COL, STOPS, OUT)
    target = jnp.concatenate([orders, spread[..., OUT:]], axis=-1)
    return jnp.stack([left_slot, right_slot, target], axis=-1).astype(jnp.int32)


def draw_pair_counts(key, part):
    first, second, third, fourth = jax.random.split(key, 4)
    shape = (N_ROW, N_COL, STOPS)
    factor_one = jax.random.randint(first, shape, 0, 3)
    factor_two = jax.random.randint(second, shape, 0, 3)
    counts = OUT + factor_one * factor_two
    busy_row = jax.random.randint(third, (STOPS,), 0, N_ROW)
    busy_col = jax.random.randint(fourth, (STOPS,), 0, N_COL)
    chosen = (jnp.arange(N_ROW)[:, None, None] == busy_row[None, None, :]) & (jnp.arange(N_COL)[None, :, None] == busy_col[None, None, :])
    return jnp.where(chosen, PAIRS, counts).astype(jnp.int32)


def level_of(key, dims, shards, smallest, top_value):
    factor_of = 1.0
    for axis_at, shards_of in shards:
        heights = jax.random.uniform(jax.random.fold_in(jax.random.fold_in(key, 6), axis_at), (shards_of,), jnp.float32, smallest / len(shards), top_value / len(shards))
        factor_of = factor_of * jnp.repeat(jnp.exp(heights), dims[axis_at] // shards_of).reshape((-1,) + (1,) * (len(dims) - 1 - axis_at))
    return factor_of


def noise(key, shape, scale, reach, cuts=(), kind=jnp.bfloat16):
    drawn = jax.random.normal(key, shape, jnp.float32) * scale
    if len(cuts) > 0:
        drawn = level_of(key, shape, cuts, -0.22, 0.18) * drawn
    return jnp.clip(drawn, min=-reach, max=reach).astype(kind)


def setup_inputs(seed: int = 0) -> dict:
    seeds = jax.random.split(jax.random.key(seed), 7)
    return {
        "density_owned": noise(seeds[0], (N_ROW, N_COL, SA, BS, BS), (4 * BS) ** -0.5, 0.125, ((0, 8), (1, 4)), jnp.float32),
        "hamilton_owned": noise(seeds[1], (N_ROW, N_COL, HB, BS, BS), 1.0, 6.0, ((0, 8), (1, 4)), jnp.float32),
        "density_route": draw_density_route(jax.random.fold_in(seeds[6], 71), 0),
        "hamilton_route": draw_hamilton_route(jax.random.fold_in(seeds[6], 71), 0),
        "pair_lists": draw_pair_lists(jax.random.fold_in(seeds[6], 71), 0),
        "pair_counts": draw_pair_counts(jax.random.fold_in(seeds[6], 71), 0),
    }


def grid_blocks(owned, route, rows, cols):
    slots = owned.shape[2]
    col_index = jnp.broadcast_to(jnp.arange(cols, dtype=jnp.int32)[None, :, None], route.shape[:3])
    target = jnp.zeros((rows, cols, slots) + owned.shape[3:], jnp.float32)
    return target.at[route[..., 0].astype(jnp.int32), col_index, route[..., 1].astype(jnp.int32)].set(owned)


def reference(density_owned, hamilton_owned, density_route, hamilton_route, pair_lists, pair_counts):
    left_grid = grid_blocks(density_owned, density_route, N_ROW, N_COL)
    half_grid = grid_blocks(hamilton_owned, hamilton_route, N_ROW, N_COL)
    right_low = jnp.concatenate([half_grid[:N_COL], half_grid[N_COL:]], axis=2)

    def one_device(index):
        grid_row = index // N_COL
        grid_col = index % N_COL
        result = jnp.zeros((OUT, BS, BS), jnp.float32)
        for stop_index in range(STOPS):
            left_tile = left_grid[grid_row, (grid_col + stop_index) % N_COL]
            right_tile = right_low[(grid_row + stop_index) % N_COL, grid_col]
            listing = pair_lists[grid_row, grid_col, stop_index]

            def add_pair(position, total, left_tile=left_tile, right_tile=right_tile, listing=listing):
                entry = listing[position]
                term = jnp.dot(left_tile[entry[0]], right_tile[entry[1]], precision=lax.Precision.HIGHEST, preferred_element_type=jnp.float32)
                return total.at[entry[2]].add(term)

            result = lax.fori_loop(0, pair_counts[grid_row, grid_col, stop_index], add_pair, result)
        return result

    flat = lax.map(one_device, jnp.arange(N_ROW * N_COL, dtype=jnp.int32))
    return flat.reshape(N_ROW, N_COL, OUT, BS, BS)
```

```python
import functools

import jax
import jax.numpy as jnp
from jax import lax
from jax.experimental import pallas as pl
from jax.experimental.pallas import tpu as pltpu
from jax.sharding import PartitionSpec as P

OUT = 4
STOPS = 3
CORES = 2


def from_behind(block, axis, distance):
    size = lax.axis_size(axis)
    return lax.ppermute(block, axis, [((i - distance) % size, i) for i in range(size)])


def split(x):
    high = x.astype(jnp.bfloat16)
    low = (x - high.astype(jnp.float32)).astype(jnp.bfloat16)
    return high, low


def product(left, right):
    lh, ll = split(left)
    rh, rl = split(right)
    dot = functools.partial(jnp.dot, preferred_element_type=jnp.float32)
    return dot(lh, rh) + (dot(lh, rl) + dot(ll, rh))


def pairs_kernel(phase, n_left, n_right, fresh, table, *refs):
    lefts = refs[:n_left]
    rights = refs[n_left:n_left + n_right]
    rest = refs[n_left + n_right:]
    if fresh:
        out, todo, lbuf, rbuf, lsem, rsem = rest
        out[...] = jnp.zeros_like(out)
    else:
        before, out, todo, lbuf, rbuf, lsem, rsem = rest
        out[...] = before[...]

    def pick(p, count):
        mine = table[5, p] == phase

        @pl.when(mine)
        def _():
            todo[count] = p
        return count + mine.astype(jnp.int32)

    count = lax.fori_loop(0, table.shape[1], pick, jnp.int32(0))

    def fetch(position, slot):
        p = todo[position]
        for k, ref in enumerate(lefts):
            @pl.when(table[0, p] == k)
            def _(ref=ref):
                pltpu.make_async_copy(ref.at[table[1, p]], lbuf.at[slot], lsem.at[slot]).start()
        for k, ref in enumerate(rights):
            @pl.when(table[2, p] == k)
            def _(ref=ref):
                pltpu.make_async_copy(ref.at[table[3, p]], rbuf.at[slot], rsem.at[slot]).start()

    @pl.when(count > 0)
    def _():
        fetch(0, 0)

    def step(position, carry):
        slot = lax.rem(position, 2)

        @pl.when(position + 1 < count)
        def _():
            fetch(position + 1, 1 - slot)
        pltpu.make_async_copy(lefts[0].at[0], lbuf.at[slot], lsem.at[slot]).wait()
        pltpu.make_async_copy(rights[0].at[0], rbuf.at[slot], rsem.at[slot]).wait()
        o = table[4, todo[position]]
        out[o] += product(lbuf[slot], rbuf[slot])
        return carry

    lax.fori_loop(0, count, step, 0)


def run_pairs(phase, table, lefts, rights, before, out_shape):
    n_left, n_right = len(lefts), len(rights)
    width = out_shape[-1]
    any_spec = pl.BlockSpec(memory_space=pl.ANY)
    whole = pl.BlockSpec(memory_space=pltpu.VMEM)
    fresh = before is None
    ins = list(lefts) + list(rights) + ([] if fresh else [before])
    specs = [any_spec] * (n_left + n_right) + ([] if fresh else [whole])
    work = 10 * width ** 3
    return pl.pallas_call(
        functools.partial(pairs_kernel, phase, n_left, n_right, fresh),
        out_shape=jax.ShapeDtypeStruct(out_shape, jnp.float32),
        grid_spec=pltpu.PrefetchScalarGridSpec(
            num_scalar_prefetch=1,
            grid=(),
            in_specs=specs,
            out_specs=whole,
            scratch_shapes=[
                pltpu.SMEM((table.shape[1],), jnp.int32),
                pltpu.VMEM((2, width, width), jnp.float32),
                pltpu.VMEM((2, width, width), jnp.float32),
                pltpu.SemaphoreType.DMA((2,)),
                pltpu.SemaphoreType.DMA((2,)),
            ],
        ),
        compiler_params=pltpu.CompilerParams(vmem_limit_bytes=32 << 20),
        cost_estimate=pl.CostEstimate(flops=6 * work, bytes_accessed=20 * width * width * 4, transcendentals=0),
        name="pairs_%d" % phase,
    )(table, *ins)


def gathered(density_owned, hamilton_owned, density_route, hamilton_route, pair_lists, pair_counts):
    rows, cols = lax.axis_size("row"), lax.axis_size("col")
    row, col = lax.axis_index("row"), lax.axis_index("col")
    left_count, half_count, width = density_owned.shape[2], hamilton_owned.shape[2], density_owned.shape[3]
    half = rows // 2
    c = CORES
    dens, ham = density_owned[0, 0], hamilton_owned[0, 0]

    def chips(moves):
        return [(a * c + k, b * c + k) for a, b in moves for k in range(c)]

    near = chips([(0, 1), (1, 0), (2, 3), (3, 2)])
    mid = chips([(1, 2), (2, 1)])
    outward = chips([(1, 0), (2, 3)])
    swap_all = [(i, i ^ 1) for i in range(rows)]
    swap_mid = [(i, i ^ 1) for i in range(c, rows - c)]
    swap_end = [(i, i ^ 1) for i in range(rows) if i < c or i >= rows - c]

    beside = lax.ppermute(ham, "row", near)
    own_x = lax.ppermute(ham, "row", swap_all)

    route_row = density_route[0, 0, :, 0]
    grid_rows = jnp.arange(rows, dtype=jnp.int32)
    goes = (route_row[None, :] == grid_rows[:, None]).astype(jnp.int32)
    order = jnp.arange(left_count, dtype=jnp.int32)[None, :]
    which = jnp.sum(goes * order, axis=1)
    label = jnp.sum(goes * (density_route[0, 0, :, 1][None, :] + 1), axis=1) - 1
    sent = dens.at[which].get(mode="promise_in_bounds")
    arrived = lax.all_to_all(sent, "row", split_axis=0, concat_axis=0, tiled=True)
    note = jnp.concatenate(
        [label[:, None], jnp.broadcast_to(hamilton_route[0, 0].reshape(1, -1), (rows, 2 * half_count))], axis=1)
    notes = lax.all_to_all(note, "row", split_axis=0, concat_axis=0, tiled=True)

    beside_x = lax.ppermute(beside, "row", swap_all)

    slot_of = notes[:, 0]
    source = jnp.sum(
        (slot_of[None, :] == jnp.arange(left_count, dtype=jnp.int32)[:, None]).astype(jnp.int32) * grid_rows[None, :], axis=1)
    tile = [lax.dynamic_slice_in_dim(arrived, source[b], 1, 0) for b in range(left_count)]
    after_two = [lax.ppermute(t, "col", [((j + 2) % cols, j) for j in range(cols)]) for t in tile]
    odd_to_even = [(j + 1, j) for j in range(0, cols, 2)]
    even_to_odd = [(j, j + 1) for j in range(0, cols, 2)]
    after_one_even = [lax.ppermute(t, "col", odd_to_even) for t in tile]
    after_one_odd = [lax.ppermute(t, "col", even_to_odd) for t in after_two]

    ham_late, _ = lax.optimization_barrier((ham, arrived[0, :8, :128]))
    far_mid, far_out, far_mid_x, far_out_x = [], [], [], []
    for f in range(2 * half_count):
        block = ham_late[f:f + 1] if f < half_count else beside[f - half_count:f - half_count + 1]
        got = lax.ppermute(block, "row", mid)
        far_mid.append(got)
        far_out.append(lax.ppermute(got, "row", outward))
    for f in range(2 * half_count):
        far_mid_x.append(lax.ppermute(far_mid[f], "row", swap_mid))
        far_out_x.append(lax.ppermute(far_out[f], "row", swap_end))

    stops, pairs = pair_lists.shape[2], pair_lists.shape[3]
    total = stops * pairs
    listing = pair_lists[0, 0].reshape(total, 3)
    stop = jnp.arange(total, dtype=jnp.int32) // pairs
    live = (jnp.arange(total, dtype=jnp.int32) % pairs) < jnp.repeat(pair_counts[0, 0], pairs, total_repeat_length=total)
    x, y, o = listing[:, 0], listing[:, 1], listing[:, 2]
    is_odd = col % 2
    group = jnp.where(stop == 0, 0, jnp.where(stop == 2, 1, 2 + is_odd))
    left_ref = group * left_count + x
    left_pos = jnp.zeros_like(left_ref)
    wanted = ((row + stop) % half + jnp.where(y >= half_count, half, 0)) * half_count + y % half_count
    routes = notes[:, 1:].reshape(rows * half_count, 2)
    target = routes[:, 0] * half_count + routes[:, 1]
    owner_code = jnp.sum(
        (target[None, :] == wanted[:, None]).astype(jnp.int32)
        * jnp.arange(rows * half_count, dtype=jnp.int32)[None, :], axis=1)
    owner, q = owner_code // half_count, owner_code % half_count
    chip, owner_chip = row // c, owner // c
    crossed = (owner % c != row % c).astype(jnp.int32)
    same = owner_chip == chip
    paired = owner_chip // 2 == chip // 2
    inner = jnp.logical_or(owner_chip == 1, owner_chip == 2)
    far_index = jnp.where(inner, 0, half_count) + q
    i_am_inner = jnp.logical_or(chip == 1, chip == 2)
    n_far = 2 * half_count
    far_ref = 4 + jnp.where(i_am_inner, 0, 2 * n_far) + crossed * n_far + far_index
    right_ref = jnp.where(same, crossed, jnp.where(paired, 2 + crossed, far_ref))
    right_pos = jnp.where(paired, q, 0)
    late = jnp.logical_and(jnp.logical_not(paired), far_index >= half_count)
    phase = jnp.where(live, late.astype(jnp.int32), -1)
    table = jnp.stack([left_ref, left_pos, right_ref, right_pos, o, phase], axis=0)

    lefts = tile + after_two + after_one_even + after_one_odd
    rights = [ham, own_x, beside, beside_x] + far_mid + far_mid_x + far_out + far_out_x
    shape = (OUT, width, width)
    early_rights = [r for r in rights[:4]] + [r for k, r in enumerate(rights[4:]) if k % n_far < half_count]
    late_rights = [r for k, r in enumerate(rights[4:]) if k % n_far >= half_count]
    block = jnp.maximum(right_ref - 4, 0)
    early_ref = jnp.where(right_ref < 4, right_ref, 4 + (block // n_far) * half_count + block % n_far)
    late_ref = (block // n_far) * half_count + block % n_far - half_count
    table = table.at[2].set(jnp.where(late, late_ref, early_ref))
    result = run_pairs(0, table, lefts, early_rights, None, shape)
    result = run_pairs(1, table, lefts, late_rights, result, shape)
    return result[None, None]


def stop_products(total, left_tile, right_tile, listing, live):

    def add_pair(position, running):
        entry = listing[position]
        left_block = lax.dynamic_index_in_dim(left_tile, entry[0], 0, keepdims=False)
        right_block = lax.dynamic_index_in_dim(right_tile, entry[1], 0, keepdims=False)
        term = jnp.dot(left_block, right_block, precision=lax.Precision.HIGHEST, preferred_element_type=jnp.float32)
        current = lax.dynamic_index_in_dim(running, entry[2], 0, keepdims=False)
        return lax.dynamic_update_index_in_dim(running, current + term, entry[2], 0)

    return lax.fori_loop(0, live, add_pair, total)


def shifted(density_owned, hamilton_owned, density_route, hamilton_route, pair_lists, pair_counts):
    rows = lax.axis_size("row")
    my_row = lax.axis_index("row")
    half = rows // 2
    left_count, half_count, width = density_owned.shape[2], hamilton_owned.shape[2], density_owned.shape[3]
    owned = jnp.concatenate([density_owned[0, 0], hamilton_owned[0, 0]], axis=0)
    targets = jnp.concatenate([density_route[0, 0, :, 0], hamilton_route[0, 0, :, 0]])
    labels = jnp.concatenate([density_route[0, 0, :, 1], hamilton_route[0, 0, :, 1] + left_count])
    send_blocks = jnp.zeros((rows, width, width), jnp.float32).at[targets].set(owned)
    send_labels = jnp.full((rows,), -1, jnp.int32).at[targets].set(labels)
    arrived, arrived_labels = (
        lax.all_to_all(send_blocks, "row", split_axis=0, concat_axis=0, tiled=True),
        lax.all_to_all(send_labels, "row", split_axis=0, concat_axis=0, tiled=True),
    )
    wanted = jnp.arange(left_count + half_count, dtype=jnp.int32)
    matches = (arrived_labels[None, :] == wanted[:, None]).astype(jnp.int32)
    sources = jnp.sum(matches * jnp.arange(rows, dtype=jnp.int32)[None, :], axis=1)
    placed = arrived[sources]
    left_tile = placed[:left_count]
    own_half = placed[left_count:]
    other_half = from_behind(own_half, "row", half)
    right_tile = jnp.where(
        my_row < half,
        jnp.concatenate([own_half, other_half], axis=0),
        jnp.concatenate([other_half, own_half], axis=0),
    )
    result = jnp.zeros((OUT, width, width), jnp.float32)
    for stop_index in range(STOPS):
        result = stop_products(
            result, left_tile, right_tile, pair_lists[0, 0, stop_index], pair_counts[0, 0, stop_index])
        if stop_index + 1 < STOPS:
            left_tile = from_behind(left_tile, "col", -1)
            right_tile = from_behind(right_tile, "row", -1)
    return result[None, None]


def solution(mesh):
    rows, cols = mesh.shape["row"], mesh.shape["col"]
    lined = rows == CORES * (STOPS + 1) and cols % 2 == 0
    return jax.shard_map(
        gathered if lined else shifted,
        mesh=mesh,
        in_specs=(
            P("row", "col", None, None, None),
            P("row", "col", None, None, None),
            P("row", "col", None, None),
            P("row", "col", None, None),
            P("row", "col", None, None, None),
            P("row", "col", None),
        ),
        out_specs=P("row", "col", None, None, None),
        check_vma=False,
    )
```

```python
import functools

import jax
import jax.numpy as jnp
from jax import lax
from jax.experimental import pallas as pl
from jax.experimental.pallas import tpu as pltpu
from jax.sharding import PartitionSpec as P


OUT = 4
STOPS = 3
LAST = 1
NOTE = 8
CORES = 2


def from_behind(block, axis, distance):
    size = lax.axis_size(axis)
    return lax.ppermute(block, axis, [((i - distance) % size, i) for i in range(size)])


def split(x):
    high = x.astype(jnp.bfloat16)
    low = (x - high.astype(jnp.float32)).astype(jnp.bfloat16)
    return high, low


def product(left, right):
    lh, ll = split(left)
    rh, rl = split(right)
    dot = functools.partial(jnp.dot, preferred_element_type=jnp.float32)
    return dot(lh, rh) + (dot(lh, rl) + dot(ll, rh))


def pairs_kernel(phase, n_left, n_right, fresh, table, *refs):
    lefts = refs[:n_left]
    rights = refs[n_left:n_left + n_right]
    rest = refs[n_left + n_right:]
    if fresh:
        out, todo, lbuf, rbuf, lsem, rsem = rest
        out[...] = jnp.zeros_like(out)
    else:
        before, out, todo, lbuf, rbuf, lsem, rsem = rest
        out[...] = before[...]

    def pick(p, count):
        mine = table[5, p] == phase

        @pl.when(mine)
        def _():
            todo[count] = p

        return count + mine.astype(jnp.int32)

    count = lax.fori_loop(0, table.shape[1], pick, jnp.int32(0))

    def fetch(position, slot):
        p = todo[position]
        for k, ref in enumerate(lefts):
            @pl.when(table[0, p] == k)
            def _(ref=ref):
                pltpu.make_async_copy(ref.at[table[1, p]], lbuf.at[slot], lsem.at[slot]).start()
        for k, ref in enumerate(rights):
            @pl.when(table[2, p] == k)
            def _(ref=ref):
                pltpu.make_async_copy(ref.at[table[3, p]], rbuf.at[slot], rsem.at[slot]).start()

    @pl.when(count > 0)
    def _():
        fetch(0, 0)

    def step(position, carry):
        slot = lax.rem(position, 2)

        @pl.when(position + 1 < count)
        def _():
            fetch(position + 1, 1 - slot)

        pltpu.make_async_copy(lefts[0].at[0], lbuf.at[slot], lsem.at[slot]).wait()
        pltpu.make_async_copy(rights[0].at[0], rbuf.at[slot], rsem.at[slot]).wait()
        o = table[4, todo[position]]
        out[o] += product(lbuf[slot], rbuf[slot])
        return carry

    lax.fori_loop(0, count, step, 0)


def run_pairs(phase, table, lefts, rights, before, out_shape):
    n_left, n_right = len(lefts), len(rights)
    width = out_shape[-1]
    any_spec = pl.BlockSpec(memory_space=pl.ANY)
    whole = pl.BlockSpec(memory_space=pltpu.VMEM)
    fresh = before is None
    ins = list(lefts) + list(rights) + ([] if fresh else [before])
    specs = [any_spec] * (n_left + n_right) + ([] if fresh else [whole])
    work = 10 * width ** 3
    return pl.pallas_call(
        functools.partial(pairs_kernel, phase, n_left, n_right, fresh),
        out_shape=jax.ShapeDtypeStruct(out_shape, jnp.float32),
        grid_spec=pltpu.PrefetchScalarGridSpec(
            num_scalar_prefetch=1,
            grid=(),
            in_specs=specs,
            out_specs=whole,
            scratch_shapes=[
                pltpu.SMEM((table.shape[1],), jnp.int32),
                pltpu.VMEM((2, width, width), jnp.float32),
                pltpu.VMEM((2, width, width), jnp.float32),
                pltpu.SemaphoreType.DMA((2,)),
                pltpu.SemaphoreType.DMA((2,)),
            ],
        ),
        compiler_params=pltpu.CompilerParams(vmem_limit_bytes=32 << 20),
        cost_estimate=pl.CostEstimate(flops=6 * work, bytes_accessed=20 * width * width * 4, transcendentals=0),
    )(table, *ins)


def pack_kernel(d_route, h_route, dens, sent, blocks, notes, in_sem, out_sem, note_sem):
    count, width = dens.shape[0], dens.shape[1]
    rows = sent.shape[0]
    for q in range(count):
        pltpu.make_async_copy(dens.at[q], blocks.at[q], in_sem.at[q]).start()
    lane = lax.broadcasted_iota(jnp.int32, notes.shape[1:], 1)
    shared = jnp.full(notes.shape[1:], -1.0, jnp.float32)
    for k in range(h_route.shape[0]):
        shared = jnp.where(lane == k + 1, h_route[k].astype(jnp.float32), shared)
    for t in range(rows):
        notes[t] = shared
    for q in range(count):
        notes[d_route[2 * q]] = jnp.where(lane == 0, d_route[2 * q + 1].astype(jnp.float32), shared)
    note_copy = pltpu.make_async_copy(notes, sent.at[:, pl.ds(width, NOTE), :], note_sem)
    note_copy.start()
    outs = []
    for q in range(count):
        pltpu.make_async_copy(dens.at[q], blocks.at[q], in_sem.at[q]).wait()
        out = pltpu.make_async_copy(blocks.at[q], sent.at[d_route[2 * q], pl.ds(0, width), :], out_sem.at[q])
        out.start()
        outs.append(out)
    for out in outs:
        out.wait()
    note_copy.wait()


def pack(d_route, h_route, dens, rows):
    count, width = dens.shape[0], dens.shape[1]
    return pl.pallas_call(
        pack_kernel,
        out_shape=jax.ShapeDtypeStruct((rows, width + NOTE, width), jnp.float32),
        grid_spec=pltpu.PrefetchScalarGridSpec(
            num_scalar_prefetch=2,
            grid=(),
            in_specs=[pl.BlockSpec(memory_space=pl.ANY)],
            out_specs=pl.BlockSpec(memory_space=pl.ANY),
            scratch_shapes=[
                pltpu.VMEM(dens.shape, jnp.float32),
                pltpu.VMEM((rows, NOTE, width), jnp.float32),
                pltpu.SemaphoreType.DMA((count,)),
                pltpu.SemaphoreType.DMA((count,)),
                pltpu.SemaphoreType.DMA,
            ],
        ),
        cost_estimate=pl.CostEstimate(flops=0, bytes_accessed=8 * count * width * width, transcendentals=0),
        name="pack",
    )(d_route, h_route, dens)


def gathered(*args):
    return gathered_product(*args)


def gathered_product(density_owned, hamilton_owned, density_route, hamilton_route, pair_lists, pair_counts):
    rows, cols = lax.axis_size("row"), lax.axis_size("col")
    row, col = lax.axis_index("row"), lax.axis_index("col")
    left_count, half_count, width = density_owned.shape[2], hamilton_owned.shape[2], density_owned.shape[3]
    half = rows // 2
    c = CORES
    dens, ham = density_owned[0, 0], hamilton_owned[0, 0]

    def chips(moves):
        return [(a * c + k, b * c + k) for a, b in moves for k in range(c)]

    inward = chips([(0, 1), (3, 2)])
    mid = chips([(1, 2), (2, 1)])
    outward = chips([(1, 0), (2, 3)])
    swap_all = [(i, i ^ 1) for i in range(rows)]
    swap_mid = [(i, i ^ 1) for i in range(c, rows - c)]
    swap_end = [(i, i ^ 1) for i in range(rows) if i < c or i >= rows - c]
    n_far = 2 * half_count

    def move(block, pairs, axis="row"):
        return lax.ppermute(block, axis, pairs)

    beside_out = move(ham, outward)
    own_x = move(ham, swap_all)

    grid_rows = jnp.arange(rows, dtype=jnp.int32)
    sent = pack(density_route[0, 0].reshape(-1), hamilton_route[0, 0].reshape(-1), dens, rows)
    arrived = lax.all_to_all(sent, "row", split_axis=0, concat_axis=0, tiled=True)
    notes = arrived[:, width, :1 + 2 * half_count].astype(jnp.int32)

    blocks = [ham[q:q + 1] for q in range(half_count)]
    beside_in = [move(block, inward) for block in blocks]
    beside_in_x = [move(block, swap_mid) for block in beside_in]
    beside_out_x = move(beside_out, swap_end)

    slot_of = notes[:, 0]
    source = jnp.sum(
        (slot_of[None, :] == jnp.arange(left_count, dtype=jnp.int32)[:, None]).astype(jnp.int32) * grid_rows[None, :], axis=1)
    tile = [lax.dynamic_slice(arrived, (source[b], 0, 0), (1, width, width)) for b in range(left_count)]
    two_on = [((j + 2) % cols, j) for j in range(cols)]
    odd_to_even = [(j + 1, j) for j in range(0, cols, 2)]
    even_to_odd = [(j, j + 1) for j in range(0, cols, 2)]
    after_two = [move(t, two_on, "col") for t in tile]
    after_one_even = [move(t, odd_to_even, "col") for t in tile]
    after_one_odd = [move(t, even_to_odd, "col") for t in after_two]

    far_mid, far_out, far_mid_x, far_out_x = [], [], [], []
    for f in range(n_far):
        far_mid.append(move((blocks + beside_in)[f], mid))
        far_out.append(move(far_mid[f], outward))
        far_mid_x.append(move(far_mid[f], swap_mid))
        far_out_x.append(move(far_out[f], swap_end))

    stops, pairs = pair_lists.shape[2], pair_lists.shape[3]
    total = stops * pairs
    listing = pair_lists[0, 0].reshape(total, 3)
    stop = jnp.arange(total, dtype=jnp.int32) // pairs
    live = (jnp.arange(total, dtype=jnp.int32) % pairs) < jnp.repeat(pair_counts[0, 0], pairs, total_repeat_length=total)
    x, y, o = listing[:, 0], listing[:, 1], listing[:, 2]
    is_odd = col % 2
    group = jnp.where(stop == 0, 0, jnp.where(stop == 2, 1, 2 + is_odd))
    left_ref = group * left_count + x
    left_pos = jnp.zeros_like(left_ref)
    wanted = ((row + stop) % half + jnp.where(y >= half_count, half, 0)) * half_count + y % half_count
    routes = notes[:, 1:].reshape(rows * half_count, 2)
    target = routes[:, 0] * half_count + routes[:, 1]
    owner_code = jnp.sum(
        (target[None, :] == wanted[:, None]).astype(jnp.int32)
        * jnp.arange(rows * half_count, dtype=jnp.int32)[None, :], axis=1)
    owner, q = owner_code // half_count, owner_code % half_count
    chip, owner_chip = row // c, owner // c
    crossed = (owner % c != row % c).astype(jnp.int32)
    same = owner_chip == chip
    paired = owner_chip // 2 == chip // 2
    inner = jnp.logical_or(owner_chip == 1, owner_chip == 2)
    far_index = jnp.where(inner, 0, half_count) + q
    i_am_inner = jnp.logical_or(chip == 1, chip == 2)
    near_refs = 4 + 2 * half_count
    far_ref = near_refs + jnp.where(i_am_inner, 0, 2 * n_far) + crossed * n_far + far_index
    beside_ref = jnp.where(i_am_inner, 4 + crossed * half_count + q, 2 + crossed)
    right_ref = jnp.where(same, crossed, jnp.where(paired, beside_ref, far_ref))
    right_pos = jnp.where(jnp.logical_and(paired, right_ref < 4), q, 0)
    cut = n_far - LAST
    late = jnp.logical_and(jnp.logical_not(paired), far_index >= cut)
    phase = jnp.where(live, late.astype(jnp.int32), -1)
    far_group, far_place = (right_ref - near_refs) // n_far, (right_ref - near_refs) % n_far
    early_ref = jnp.where(right_ref < near_refs, right_ref, near_refs + far_group * cut + far_place)
    late_ref = far_group * LAST + far_place - cut
    table = jnp.stack([left_ref, left_pos, jnp.where(late, late_ref, early_ref), right_pos, o, phase], axis=0)

    lefts = tile + after_two + after_one_even + after_one_odd
    far = [far_mid, far_mid_x, far_out, far_out_x]
    early_rights = [ham, own_x, beside_out, beside_out_x] + beside_in + beside_in_x + [r for g in far for r in g[:cut]]
    late_rights = [r for g in far for r in g[cut:]]
    shape = (OUT, width, width)
    result = run_pairs(0, table, lefts, early_rights, None, shape)
    result = run_pairs(1, table, lefts, late_rights, result, shape)
    return result[None, None]


def stop_products(total, left_tile, right_tile, listing, live):

    def add_pair(position, running):
        entry = listing[position]
        left_block = lax.dynamic_index_in_dim(left_tile, entry[0], 0, keepdims=False)
        right_block = lax.dynamic_index_in_dim(right_tile, entry[1], 0, keepdims=False)
        term = jnp.dot(left_block, right_block, precision=lax.Precision.HIGHEST, preferred_element_type=jnp.float32)
        current = lax.dynamic_index_in_dim(running, entry[2], 0, keepdims=False)
        return lax.dynamic_update_index_in_dim(running, current + term, entry[2], 0)

    return lax.fori_loop(0, live, add_pair, total)


def shifted(density_owned, hamilton_owned, density_route, hamilton_route, pair_lists, pair_counts):
    rows = lax.axis_size("row")
    my_row = lax.axis_index("row")
    half = rows // 2
    left_count, half_count, width = density_owned.shape[2], hamilton_owned.shape[2], density_owned.shape[3]
    owned = jnp.concatenate([density_owned[0, 0], hamilton_owned[0, 0]], axis=0)
    targets = jnp.concatenate([density_route[0, 0, :, 0], hamilton_route[0, 0, :, 0]])
    labels = jnp.concatenate([density_route[0, 0, :, 1], hamilton_route[0, 0, :, 1] + left_count])
    send_blocks = jnp.zeros((rows, width, width), jnp.float32).at[targets].set(owned)
    send_labels = jnp.full((rows,), -1, jnp.int32).at[targets].set(labels)
    arrived, arrived_labels = (
        lax.all_to_all(send_blocks, "row", split_axis=0, concat_axis=0, tiled=True),
        lax.all_to_all(send_labels, "row", split_axis=0, concat_axis=0, tiled=True),
    )
    wanted = jnp.arange(left_count + half_count, dtype=jnp.int32)
    matches = (arrived_labels[None, :] == wanted[:, None]).astype(jnp.int32)
    sources = jnp.sum(matches * jnp.arange(rows, dtype=jnp.int32)[None, :], axis=1)
    placed = arrived[sources]
    left_tile = placed[:left_count]
    own_half = placed[left_count:]
    other_half = from_behind(own_half, "row", half)
    right_tile = jnp.where(
        my_row < half,
        jnp.concatenate([own_half, other_half], axis=0),
        jnp.concatenate([other_half, own_half], axis=0),
    )
    result = jnp.zeros((OUT, width, width), jnp.float32)
    for stop_index in range(STOPS):
        result = stop_products(
            result, left_tile, right_tile, pair_lists[0, 0, stop_index], pair_counts[0, 0, stop_index])
        if stop_index + 1 < STOPS:
            left_tile = from_behind(left_tile, "col", -1)
            right_tile = from_behind(right_tile, "row", -1)
    return result[None, None]


def solution(mesh):
    rows, cols = mesh.shape["row"], mesh.shape["col"]
    lined = rows == CORES * (STOPS + 1) and cols % 2 == 0
    return jax.shard_map(
        gathered if lined else shifted,
        mesh=mesh,
        in_specs=(
            P("row", "col", None, None, None),
            P("row", "col", None, None, None),
            P("row", "col", None, None),
            P("row", "col", None, None),
            P("row", "col", None, None, None),
            P("row", "col", None),
        ),
        out_specs=P("row", "col", None, None, None),
        check_vma=False,
    )
```

```python
import functools

import jax
import jax.numpy as jnp
from jax import lax
from jax.experimental import pallas as pl
from jax.experimental.pallas import tpu as pltpu
from jax.sharding import PartitionSpec as P


OUT = 4
STOPS = 3
NOTE = 8
CORES = 2


def from_behind(block, axis, distance):
    size = lax.axis_size(axis)
    return lax.ppermute(block, axis, [((i - distance) % size, i) for i in range(size)])


def split(x):
    high = x.astype(jnp.bfloat16)
    low = (x - high.astype(jnp.float32)).astype(jnp.bfloat16)
    return high, low


def product(left, right):
    lh, ll = split(left)
    rh, rl = split(right)
    dot = functools.partial(jnp.dot, preferred_element_type=jnp.float32)
    return dot(lh, rh) + (dot(lh, rl) + dot(ll, rh))


def pairs_kernel(phase, n_left, n_right, fresh, table, *refs):
    lefts = refs[:n_left]
    rights = refs[n_left:n_left + n_right]
    rest = refs[n_left + n_right:]
    before, rest = (None, rest) if fresh else (rest[0], rest[1:])
    out, todo, used, acc, lbuf, rbuf, lsem, rsem, asem = rest
    slots = acc.shape[0]
    for o in range(slots):
        used[o] = jnp.int32(1 if fresh else 0)

    def pick(p, count):
        mine = table[5, p] == phase

        @pl.when(mine)
        def _():
            todo[count] = p
            used[table[4, p]] = jnp.int32(1)

        return count + mine.astype(jnp.int32)

    count = lax.fori_loop(0, table.shape[1], pick, jnp.int32(0))

    def fetch(position, slot):
        p = todo[position]
        for k, ref in enumerate(lefts):
            @pl.when(table[0, p] == k)
            def _(ref=ref):
                pltpu.make_async_copy(ref.at[0], lbuf.at[slot], lsem.at[slot]).start()
        for k, ref in enumerate(rights):
            @pl.when(table[2, p] == k)
            def _(ref=ref):
                pltpu.make_async_copy(ref.at[table[3, p]], rbuf.at[slot], rsem.at[slot]).start()

    @pl.when(count > 0)
    def _():
        fetch(0, 0)

    if fresh:
        acc[...] = jnp.zeros_like(acc)
    else:
        for o in range(slots):
            @pl.when(used[o] == 1)
            def _(o=o):
                pltpu.make_async_copy(before.at[o], acc.at[o], asem.at[o]).start()
        for o in range(slots):
            @pl.when(used[o] == 1)
            def _(o=o):
                pltpu.make_async_copy(before.at[o], acc.at[o], asem.at[o]).wait()

    def step(position, carry):
        slot = lax.rem(position, 2)

        @pl.when(position + 1 < count)
        def _():
            fetch(position + 1, 1 - slot)

        pltpu.make_async_copy(lefts[0].at[0], lbuf.at[slot], lsem.at[slot]).wait()
        pltpu.make_async_copy(rights[0].at[0], rbuf.at[slot], rsem.at[slot]).wait()
        o = table[4, todo[position]]
        acc[o] += product(lbuf[slot], rbuf[slot])
        return carry

    lax.fori_loop(0, count, step, 0)
    for o in range(slots):
        @pl.when(used[o] == 1)
        def _(o=o):
            pltpu.make_async_copy(acc.at[o], out.at[o], asem.at[o]).start()
    for o in range(slots):
        @pl.when(used[o] == 1)
        def _(o=o):
            pltpu.make_async_copy(acc.at[o], out.at[o], asem.at[o]).wait()


def run_pairs(phase, table, lefts, rights, before, out_shape):
    n_left, n_right = len(lefts), len(rights)
    slots, width = out_shape[0], out_shape[-1]
    fresh = before is None
    ins = list(lefts) + list(rights) + ([] if fresh else [before])
    any_spec = pl.BlockSpec(memory_space=pl.ANY)
    block = 4 * width * width
    return pl.pallas_call(
        functools.partial(pairs_kernel, phase, n_left, n_right, fresh),
        out_shape=jax.ShapeDtypeStruct(out_shape, jnp.float32),
        grid_spec=pltpu.PrefetchScalarGridSpec(
            num_scalar_prefetch=1,
            grid=(),
            in_specs=[any_spec] * len(ins),
            out_specs=any_spec,
            scratch_shapes=[
                pltpu.SMEM((table.shape[1],), jnp.int32),
                pltpu.SMEM((slots,), jnp.int32),
                pltpu.VMEM(out_shape, jnp.float32),
                pltpu.VMEM((2, width, width), jnp.float32),
                pltpu.VMEM((2, width, width), jnp.float32),
                pltpu.SemaphoreType.DMA((2,)),
                pltpu.SemaphoreType.DMA((2,)),
                pltpu.SemaphoreType.DMA((slots,)),
            ],
        ),
        input_output_aliases={} if fresh else {len(ins): 0},
        compiler_params=pltpu.CompilerParams(vmem_limit_bytes=32 << 20),
        cost_estimate=pl.CostEstimate(flops=60 * width ** 3, bytes_accessed=20 * block, transcendentals=0),
    )(table, *ins)


def pack_kernel(d_route, h_route, dens, sent, blocks, notes, in_sem, out_sem, note_sem):
    count, width = dens.shape[0], dens.shape[1]
    rows = sent.shape[0]
    for q in range(count):
        pltpu.make_async_copy(dens.at[q], blocks.at[q], in_sem.at[q]).start()
    lane = lax.broadcasted_iota(jnp.int32, notes.shape[1:], 1)
    shared = jnp.full(notes.shape[1:], -1.0, jnp.float32)
    for k in range(h_route.shape[0]):
        shared = jnp.where(lane == k + 1, h_route[k].astype(jnp.float32), shared)
    for t in range(rows):
        notes[t] = shared
    for q in range(count):
        notes[d_route[2 * q]] = jnp.where(lane == 0, d_route[2 * q + 1].astype(jnp.float32), shared)
    note_copy = pltpu.make_async_copy(notes, sent.at[:, pl.ds(width, NOTE), :], note_sem)
    note_copy.start()
    outs = []
    for q in range(count):
        pltpu.make_async_copy(dens.at[q], blocks.at[q], in_sem.at[q]).wait()
        out = pltpu.make_async_copy(blocks.at[q], sent.at[d_route[2 * q], pl.ds(0, width), :], out_sem.at[q])
        out.start()
        outs.append(out)
    for out in outs:
        out.wait()
    note_copy.wait()


def pack(d_route, h_route, dens, rows):
    count, width = dens.shape[0], dens.shape[1]
    return pl.pallas_call(
        pack_kernel,
        out_shape=jax.ShapeDtypeStruct((rows, width + NOTE, width), jnp.float32),
        grid_spec=pltpu.PrefetchScalarGridSpec(
            num_scalar_prefetch=2,
            grid=(),
            in_specs=[pl.BlockSpec(memory_space=pl.ANY)],
            out_specs=pl.BlockSpec(memory_space=pl.ANY),
            scratch_shapes=[
                pltpu.VMEM(dens.shape, jnp.float32),
                pltpu.VMEM((rows, NOTE, width), jnp.float32),
                pltpu.SemaphoreType.DMA((count,)),
                pltpu.SemaphoreType.DMA((count,)),
                pltpu.SemaphoreType.DMA,
            ],
        ),
        cost_estimate=pl.CostEstimate(flops=0, bytes_accessed=8 * count * width * width, transcendentals=0),
        name="pack",
    )(d_route, h_route, dens)


def gathered(*args):
    return gathered_product(*args)


def gathered_product(density_owned, hamilton_owned, density_route, hamilton_route, pair_lists, pair_counts):
    rows, cols = lax.axis_size("row"), lax.axis_size("col")
    row, col = lax.axis_index("row"), lax.axis_index("col")
    left_count, half_count, width = density_owned.shape[2], hamilton_owned.shape[2], density_owned.shape[3]
    half = rows // 2
    c = CORES
    dens, ham = density_owned[0, 0], hamilton_owned[0, 0]

    def chips(moves):
        return [(a * c + k, b * c + k) for a, b in moves for k in range(c)]

    inward = chips([(0, 1), (3, 2)])
    mid = chips([(1, 2), (2, 1)])
    outward = chips([(1, 0), (2, 3)])
    swap_all = [(i, i ^ 1) for i in range(rows)]
    swap_mid = [(i, i ^ 1) for i in range(c, rows - c)]
    swap_end = [(i, i ^ 1) for i in range(rows) if i < c or i >= rows - c]
    n_far = 2 * half_count

    def move(block, pairs, axis="row"):
        return lax.ppermute(block, axis, pairs)

    beside_out = move(ham, outward)
    own_x = move(ham, swap_all)

    grid_rows = jnp.arange(rows, dtype=jnp.int32)
    sent = pack(density_route[0, 0].reshape(-1), hamilton_route[0, 0].reshape(-1), dens, rows)
    arrived = lax.all_to_all(sent, "row", split_axis=0, concat_axis=0, tiled=True)
    notes = arrived[:, width, :1 + 2 * half_count].astype(jnp.int32)

    blocks = [ham[q:q + 1] for q in range(half_count)]
    beside_in = [move(block, inward) for block in blocks]
    beside_in_x = [move(block, swap_mid) for block in beside_in]
    beside_out_x = move(beside_out, swap_end)

    slot_of = notes[:, 0]
    source = jnp.sum(
        (slot_of[None, :] == jnp.arange(left_count, dtype=jnp.int32)[:, None]).astype(jnp.int32) * grid_rows[None, :], axis=1)
    tile = [lax.dynamic_slice(arrived, (source[b], 0, 0), (1, width, width)) for b in range(left_count)]
    two_on = [((j + 2) % cols, j) for j in range(cols)]
    odd_to_even = [(j + 1, j) for j in range(0, cols, 2)]
    even_to_odd = [(j, j + 1) for j in range(0, cols, 2)]
    after_two = [move(t, two_on, "col") for t in tile]
    after_one_even = [move(t, odd_to_even, "col") for t in tile]
    after_one_odd = [move(t, even_to_odd, "col") for t in after_two]

    far_mid, far_out, far_mid_x, far_out_x = [], [], [], []
    for f in range(n_far):
        far_mid.append(move((blocks + beside_in)[f], mid))
        far_out.append(move(far_mid[f], outward))
        far_mid_x.append(move(far_mid[f], swap_mid))
        far_out_x.append(move(far_out[f], swap_end))

    stops, pairs = pair_lists.shape[2], pair_lists.shape[3]
    total = stops * pairs
    listing = pair_lists[0, 0].reshape(total, 3)
    stop = jnp.arange(total, dtype=jnp.int32) // pairs
    live = (jnp.arange(total, dtype=jnp.int32) % pairs) < jnp.repeat(pair_counts[0, 0], pairs, total_repeat_length=total)
    x, y, o = listing[:, 0], listing[:, 1], listing[:, 2]
    is_odd = col % 2
    group = jnp.where(stop == 0, 0, jnp.where(stop == 2, 1, 2 + is_odd))
    left_ref = group * left_count + x
    left_pos = jnp.zeros_like(left_ref)
    wanted = ((row + stop) % half + jnp.where(y >= half_count, half, 0)) * half_count + y % half_count
    routes = notes[:, 1:].reshape(rows * half_count, 2)
    target = routes[:, 0] * half_count + routes[:, 1]
    owner_code = jnp.sum(
        (target[None, :] == wanted[:, None]).astype(jnp.int32)
        * jnp.arange(rows * half_count, dtype=jnp.int32)[None, :], axis=1)
    owner, q = owner_code // half_count, owner_code % half_count
    chip, owner_chip = row // c, owner // c
    crossed = (owner % c != row % c).astype(jnp.int32)
    same = owner_chip == chip
    paired = owner_chip // 2 == chip // 2
    inner = jnp.logical_or(owner_chip == 1, owner_chip == 2)
    far_index = jnp.where(inner, 0, half_count) + q
    i_am_inner = jnp.logical_or(chip == 1, chip == 2)
    near_refs = 4 + 2 * half_count
    far_ref = near_refs + jnp.where(i_am_inner, 0, 2 * n_far) + crossed * n_far + far_index
    beside_ref = jnp.where(i_am_inner, 4 + crossed * half_count + q, 2 + crossed)
    right_ref = jnp.where(same, crossed, jnp.where(paired, beside_ref, far_ref))
    right_pos = jnp.where(jnp.logical_and(paired, right_ref < 4), q, 0)
    cuts = (half_count, n_far - 1)
    is_far = jnp.logical_not(paired)
    far_group, far_place = (right_ref - near_refs) // n_far, (right_ref - near_refs) % n_far
    first = jnp.logical_and(stop != 1, jnp.logical_or(paired, far_index < cuts[0]))
    late = jnp.logical_and(is_far, far_index >= cuts[1])
    phase = jnp.where(live, jnp.where(late, 2, jnp.where(first, 0, 1)), -1)
    near_or = lambda cut: jnp.where(is_far, near_refs + far_group * cut + far_place, right_ref)
    last_ref = far_group * (n_far - cuts[1]) + far_place - cuts[1]
    right_ref = jnp.where(late, last_ref, jnp.where(first, near_or(cuts[0]), near_or(cuts[1])))
    table = jnp.stack([left_ref, left_pos, right_ref, right_pos, o, phase], axis=0)

    lefts = tile + after_two + after_one_even + after_one_odd
    near = [ham, own_x, beside_out, beside_out_x] + beside_in + beside_in_x
    far = [far_mid, far_mid_x, far_out, far_out_x]
    shape = (OUT, width, width)
    result = run_pairs(0, table, tile + after_two, near + [r for g in far for r in g[:cuts[0]]], None, shape)
    result = run_pairs(1, table, lefts, near + [r for g in far for r in g[:cuts[1]]], result, shape)
    result = run_pairs(2, table, lefts, [r for g in far for r in g[cuts[1]:]], result, shape)
    return result[None, None]


def stop_products(total, left_tile, right_tile, listing, live):

    def add_pair(position, running):
        entry = listing[position]
        left_block = lax.dynamic_index_in_dim(left_tile, entry[0], 0, keepdims=False)
        right_block = lax.dynamic_index_in_dim(right_tile, entry[1], 0, keepdims=False)
        term = jnp.dot(left_block, right_block, precision=lax.Precision.HIGHEST, preferred_element_type=jnp.float32)
        current = lax.dynamic_index_in_dim(running, entry[2], 0, keepdims=False)
        return lax.dynamic_update_index_in_dim(running, current + term, entry[2], 0)

    return lax.fori_loop(0, live, add_pair, total)


def shifted(density_owned, hamilton_owned, density_route, hamilton_route, pair_lists, pair_counts):
    rows = lax.axis_size("row")
    my_row = lax.axis_index("row")
    half = rows // 2
    left_count, half_count, width = density_owned.shape[2], hamilton_owned.shape[2], density_owned.shape[3]
    owned = jnp.concatenate([density_owned[0, 0], hamilton_owned[0, 0]], axis=0)
    targets = jnp.concatenate([density_route[0, 0, :, 0], hamilton_route[0, 0, :, 0]])
    labels = jnp.concatenate([density_route[0, 0, :, 1], hamilton_route[0, 0, :, 1] + left_count])
    send_blocks = jnp.zeros((rows, width, width), jnp.float32).at[targets].set(owned)
    send_labels = jnp.full((rows,), -1, jnp.int32).at[targets].set(labels)
    arrived, arrived_labels = (
        lax.all_to_all(send_blocks, "row", split_axis=0, concat_axis=0, tiled=True),
        lax.all_to_all(send_labels, "row", split_axis=0, concat_axis=0, tiled=True),
    )
    wanted = jnp.arange(left_count + half_count, dtype=jnp.int32)
    matches = (arrived_labels[None, :] == wanted[:, None]).astype(jnp.int32)
    sources = jnp.sum(matches * jnp.arange(rows, dtype=jnp.int32)[None, :], axis=1)
    placed = arrived[sources]
    left_tile = placed[:left_count]
    own_half = placed[left_count:]
    other_half = from_behind(own_half, "row", half)
    right_tile = jnp.where(
        my_row < half,
        jnp.concatenate([own_half, other_half], axis=0),
        jnp.concatenate([other_half, own_half], axis=0),
    )
    result = jnp.zeros((OUT, width, width), jnp.float32)
    for stop_index in range(STOPS):
        result = stop_products(
            result, left_tile, right_tile, pair_lists[0, 0, stop_index], pair_counts[0, 0, stop_index])
        if stop_index + 1 < STOPS:
            left_tile = from_behind(left_tile, "col", -1)
            right_tile = from_behind(right_tile, "row", -1)
    return result[None, None]


def solution(mesh):
    rows, cols = mesh.shape["row"], mesh.shape["col"]
    lined = rows == CORES * (STOPS + 1) and cols % 2 == 0
    return jax.shard_map(
        gathered if lined else shifted,
        mesh=mesh,
        in_specs=(
            P("row", "col", None, None, None),
            P("row", "col", None, None, None),
            P("row", "col", None, None),
            P("row", "col", None, None),
            P("row", "col", None, None, None),
            P("row", "col", None),
        ),
        out_specs=P("row", "col", None, None, None),
        check_vma=False,
    )
```
